32 devices in a mesh: grp: 2 (over x), wave: 16 (over z, y, core).
Axes of the slice: x: 2, y: 2, z: 4, core: 2. Of those that a mesh axis runs over, the one named last changes fastest.
Arguments:
- north_rows: bfloat16 [2560, 128, 274], P(('grp', 'wave')), parts along dimension 0, may hold values from -6 to 6
- south_rows: bfloat16 [2560, 128, 274], P(('grp', 'wave')), parts along dimension 0, may hold values from -6 to 6
- lon_counts: int32 [1280], replicated, may hold values from 20 to 5148, as said below
- slot_wave: int32 [128], replicated, may hold values from 0 to 2559, as said below
- legendre: bfloat16 [128, 1280, 1280], P('wave'), may hold values from -0.15625 to 0.15625
- mode_rates: float32 [137], replicated, may hold values from 0.05 to 20
- to_modes: bfloat16 [137, 137], replicated, may hold values from -0.5 to 0.5
- from_modes: bfloat16 [137, 137], replicated, may hold values from -0.5 to 0.5
Outputs:
- spec_state: bfloat16 [256, 1280, 274], P(('grp', 'wave')), parts along dimension 0
- new_rows: bfloat16 [2560, 128, 274], P(('grp', 'wave')), parts along dimension 0
The draws below stay inside these ranges and needn't reach their ends.
There are 2 independent parts, one for each index of `grp`. The reference program is written for one: setup_inputs(seed, part) draws one part's arguments, and reference() takes and returns one part's arrays. A program takes and returns all parts, laid end to end along the dimension named above; an argument that names none is the same for every part. Nothing has to cross between parts.
Inputs may be any that keep to these rules, and one draw needn't show every extreme that they name: Wavenumber m is present in latitude row j only if 2 m is below lon_counts[j]. `slot_wave`: distinct zonal wavenumbers.
All inputs are finite; a program needn't handle non-finite values.
Results may differ from the reference program's by a relative error of at most 0.0065.
Values may be sent and summed in bfloat16 or wider, within the bound.
A program may use at most 192 MiB of HBM per device.

```python
import math
import jax
import jax.numpy as jnp
from jax import lax

NLAT = 1280
NMAX = 2559
LEV = 137
MW = 128
NS = 1280


def draw_lon_counts(key, part):
    jitter = jax.random.randint(jax.random.fold_in(key, 11), (NLAT,), 0, 4)
    jitter = jitter.at[0].set(0).at[NLAT - 1].set(3)
    row_number = jnp.arange(NLAT, dtype=jnp.int32) + 1
    return (16 + 2 * row_number * (NMAX + 1) // NLAT + 4 * jitter).astype(jnp.int32)


def draw_slot_wave(key, part):
    inner = jax.random.permutation(jax.random.fold_in(key, 21), NMAX - 1)[:MW - 2] + 1
    values = jnp.concatenate([jnp.array([0, NMAX], dtype=jnp.int32), inner.astype(jnp.int32)])
    placing = jax.random.permutation(jax.random.fold_in(key, 22), MW)
    return values[placing].astype(jnp.int32)


def shard_levels(key, dims, split, least, top_value):
    level = 1.0
    for position, shards_of in split:
        draws = jax.random.uniform(jax.random.fold_in(jax.random.fold_in(key, 6), position), (shards_of,), jnp.float32, least / len(split), top_value / len(split))
        level = level * jnp.repeat(jnp.exp(draws), dims[position] // shards_of).reshape((-1,) + (1,) * (len(dims) - 1 - position))
    return level


def normal_values(own_key, shape, spread, most, pieces=(), kind=jnp.bfloat16):
    entries = spread * jax.random.normal(own_key, shape, jnp.float32)
    if pieces:
        entries = entries * shard_levels(own_key, shape, pieces, -0.22, 0.18)
    return jnp.clip(entries, -most, most).astype(kind)


def setup_inputs(seed: int = 0, part: int = 0) -> dict:
    arg_keys = jax.random.split(jax.random.key(seed), 9)
    part_keys = jax.random.split(jax.random.fold_in(arg_keys[8], part), 9)
    return {
        "north_rows": normal_values(part_keys[0], (NLAT, MW, 2 * LEV), 1.0, 6.0, ((0, 16),)),
        "south_rows": normal_values(part_keys[1], (NLAT, MW, 2 * LEV), 1.0, 6.0, ((0, 16),)),
        "lon_counts": draw_lon_counts(jax.random.fold_in(arg_keys[8], 71), part),
        "slot_wave": draw_slot_wave(jax.random.fold_in(arg_keys[8], 71), part),
        "legendre": normal_values(arg_keys[4], (MW, NS, NLAT), NLAT ** -0.5, 0.15625, ((0, 16),)),
        "mode_rates": jnp.clip(jnp.exp(jax.random.uniform(arg_keys[5], (LEV,), jnp.float32, math.log(0.05), math.log(20.0))), 0.05, 20.0),
        "to_modes": normal_values(arg_keys[6], (LEV, LEV), LEV ** -0.5, 0.5),
        "from_modes": normal_values(arg_keys[7], (LEV, LEV), LEV ** -0.5, 0.5),
    }


def vertical_step(direct, own_waves, mode_rates, to_modes, from_modes):
    slot_count, row_total, channels = direct.shape
    levels = to_modes.shape[0]
    modal_part = jnp.dot(direct.reshape(-1, levels), to_modes, preferred_element_type=jnp.float32)
    modal_part = modal_part.reshape(slot_count, row_total, 2, levels)
    degree = own_waves[:, None] + 2 * jnp.arange(row_total, dtype=jnp.int32)[None, :]
    degree_f = degree.astype(jnp.float32)
    scaled_degree = degree_f * (degree_f + 1.0) / float(NMAX * (NMAX + 1))
    divisor = 1.0 + mode_rates[None, None, None, :] * scaled_degree[:, :, None, None]
    scaled = (modal_part / divisor).astype(jnp.bfloat16).reshape(-1, levels)
    result = jnp.dot(scaled, from_modes, preferred_element_type=jnp.float32)
    result = result.reshape(slot_count, row_total, channels)
    return jnp.where((degree <= NMAX)[:, :, None], result, 0.0).astype(jnp.bfloat16)


def reference(north_rows, south_rows, lon_counts, slot_wave, legendre, mode_rates, to_modes, from_modes):
    live_mask = 2 * slot_wave[None, :] < lon_counts[:, None]
    summed = north_rows.astype(jnp.float32) + south_rows.astype(jnp.float32)
    symmetric = jnp.where(live_mask[:, :, None], summed, 0.0).astype(jnp.bfloat16)

    def one_slot(inputs):
        wavenumber, matrix, slot_rows, live_column = inputs
        direct = jnp.dot(matrix, slot_rows, preferred_element_type=jnp.float32).astype(jnp.bfloat16)
        state = vertical_step(direct[None], wavenumber[None], mode_rates, to_modes, from_modes)[0]
        returned = lax.dot_general(matrix, state, (((0,), (0,)), ((), ())), preferred_element_type=jnp.float32)
        returned = jnp.where(live_column[:, None], returned, 0.0).astype(jnp.bfloat16)
        return state, returned

    spec_state, returned = lax.map(one_slot, (slot_wave, legendre, jnp.moveaxis(symmetric, 1, 0), live_mask.T))
    return spec_state, jnp.moveaxis(returned, 0, 1)
```

```python
import functools

import jax
import jax.numpy as jnp
from jax import lax
from jax.experimental import pallas as pl
from jax.experimental.pallas import tpu as pltpu
from jax.sharding import PartitionSpec as P

NMAX = 2559
VMEM_LIMIT = 60 * 1024 * 1024


def sum_kernel(counts_ref, waves_ref, north_ref, south_ref, out_ref):
    live = 2 * waves_ref[...] < counts_ref[...]
    total = north_ref[...].astype(jnp.float32) + south_ref[...].astype(jnp.float32)
    out_ref[...] = jnp.where(live[None], total, 0.0).astype(jnp.bfloat16)


def symmetric_part(part, levels, north, south, counts, waves):
    _, lats, slots = north.shape
    step = next((t for t in (16, 8) if lats % t == 0), lats)
    return pl.pallas_call(
        sum_kernel,
        grid=(lats // step,),
        in_specs=[
            pl.BlockSpec((step, 1), lambda g: (g, 0)),
            pl.BlockSpec((1, slots), lambda g: (0, 0)),
            pl.BlockSpec((levels, step, slots), lambda g: (part, g, 0)),
            pl.BlockSpec((levels, step, slots), lambda g: (part, g, 0)),
        ],
        out_specs=pl.BlockSpec((levels, step, slots), lambda g: (0, g, 0)),
        out_shape=jax.ShapeDtypeStruct((levels, lats, slots), jnp.bfloat16),
        name=f"sum{part}",
    )(counts, waves, north, south)


def pack_kernel(own, lats, in_ref, out_ref):
    for i in range(own):
        out_ref[0, :, lats * i : lats * (i + 1)] = in_ref[i]


def pack(rows, own):
    slots, levels, lats = rows.shape
    return pl.pallas_call(
        functools.partial(pack_kernel, own, lats),
        grid=(slots // own,),
        in_specs=[pl.BlockSpec((own, levels, lats), lambda d: (d, 0, 0))],
        out_specs=pl.BlockSpec((1, levels, own * lats), lambda d: (d, 0, 0)),
        out_shape=jax.ShapeDtypeStruct((slots // own, levels, own * lats), jnp.bfloat16),
        name="pack",
    )(rows)


def unpack_kernel(own, lats, in_ref, out_ref):
    for i in range(own):
        out_ref[i] = in_ref[0, :, lats * i : lats * (i + 1)]


def unpack(packed, own):
    senders, levels, width = packed.shape
    lats = width // own
    return pl.pallas_call(
        functools.partial(unpack_kernel, own, lats),
        grid=(senders,),
        in_specs=[pl.BlockSpec((1, levels, width), lambda d: (d, 0, 0))],
        out_specs=pl.BlockSpec((own, levels, lats), lambda d: (d, 0, 0)),
        out_shape=jax.ShapeDtypeStruct((senders * own, levels, lats), jnp.bfloat16),
        name="unpack",
    )(packed)


def compute_kernel(
    own, senders, lats, waves_ref, counts_ref, rates_ref, to_ref, from_ref, rows_ref, leg_ref,
    state_ref, back_ref, columns, returned,
):
    slot = pl.program_id(0)

    @pl.when(slot == 0)
    def _():
        for s in range(own):
            for d in range(senders):
                columns[s, :, lats * d : lats * (d + 1)] = rows_ref[d, :, lats * s : lats * (s + 1)]

    wave = waves_ref[slot]
    direct = lax.dot_general(
        columns[slot], leg_ref[0], (((1,), (1,)), ((), ())), preferred_element_type=jnp.float32
    ).astype(jnp.bfloat16)
    modal = jnp.dot(to_ref[...], direct, preferred_element_type=jnp.float32)
    degree = wave + 2 * lax.broadcasted_iota(jnp.int32, (1, leg_ref.shape[1]), 1)
    degree_f = degree.astype(jnp.float32)
    scaled_degree = degree_f * (degree_f + 1.0) / float(NMAX * (NMAX + 1))
    divisor = 1.0 + rates_ref[...] * scaled_degree
    scaled = (modal / divisor).astype(jnp.bfloat16)
    state = jnp.dot(from_ref[...], scaled, preferred_element_type=jnp.float32)
    state = jnp.where(degree <= NMAX, state, 0.0).astype(jnp.bfloat16)
    state_ref[0] = state
    back = jnp.dot(state, leg_ref[0], preferred_element_type=jnp.float32)
    returned[slot] = jnp.where(2 * wave < counts_ref[...], back, 0.0).astype(jnp.bfloat16)

    @pl.when(slot == own - 1)
    def _():
        for s in range(own):
            for d in range(senders):
                back_ref[d, :, lats * s : lats * (s + 1)] = returned[s, :, lats * d : lats * (d + 1)]


def compute(rows, legendre, own_waves, counts, rates, to_t, from_t):
    senders, levels, width = rows.shape
    own, row_total, lat_total = legendre.shape
    lats = lat_total // senders
    whole = lambda *shape: pl.BlockSpec(shape, lambda s, w: (0,) * len(shape))
    return pl.pallas_call(
        functools.partial(compute_kernel, own, senders, lats),
        grid_spec=pltpu.PrefetchScalarGridSpec(
            num_scalar_prefetch=1,
            grid=(own,),
            in_specs=[
                whole(1, lat_total),
                whole(levels, 1),
                whole(levels, levels),
                whole(levels, levels),
                whole(senders, levels, width),
                pl.BlockSpec((1, row_total, lat_total), lambda s, w: (s, 0, 0)),
            ],
            out_specs=[
                pl.BlockSpec((1, levels, row_total), lambda s, w: (s, 0, 0)),
                whole(senders, levels, width),
            ],
            scratch_shapes=[
                pltpu.VMEM((own, levels, lat_total), jnp.bfloat16),
                pltpu.VMEM((own, levels, lat_total), jnp.bfloat16),
            ],
        ),
        out_shape=[
            jax.ShapeDtypeStruct((own, levels, row_total), jnp.bfloat16),
            jax.ShapeDtypeStruct((senders, levels, width), jnp.bfloat16),
        ],
        compiler_params=pltpu.CompilerParams(vmem_limit_bytes=VMEM_LIMIT),
        cost_estimate=pl.CostEstimate(
            flops=8 * own * row_total * lat_total * levels,
            bytes_accessed=2 * own * row_total * lat_total,
            transcendentals=0,
        ),
        name="legendre",
    )(own_waves, counts, rates, to_t, from_t, rows, legendre)


def per_device(
    north_rows, south_rows, lon_counts, slot_wave, legendre, mode_rates, to_modes, from_modes
):
    lat_dev = north_rows.shape[0]
    slot_dev, row_total, lat_total = legendre.shape
    levels = to_modes.shape[0]
    my_index = lax.axis_index("wave")
    own_waves = lax.dynamic_slice_in_dim(slot_wave, my_index * slot_dev, slot_dev)
    local_counts = lax.dynamic_slice_in_dim(lon_counts, my_index * lat_dev, lat_dev)
    north = jnp.transpose(north_rows, (2, 0, 1))
    south = jnp.transpose(south_rows, (2, 0, 1))
    counts_here, waves_all = local_counts[:, None], slot_wave[None, :]
    counts_all, rates = lon_counts[None, :], mode_rates[:, None]
    to_t, from_t = to_modes.T, from_modes.T
    states, outs = [], []
    for part in range(2):
        rows = symmetric_part(part, levels, north, south, counts_here, waves_all)
        packed = pack(jnp.transpose(rows, (2, 0, 1)), slot_dev)
        moved = lax.all_to_all(packed, "wave", split_axis=0, concat_axis=0, tiled=True)
        state, back = compute(moved, legendre, own_waves, counts_all, rates, to_t, from_t)
        home = lax.all_to_all(back, "wave", split_axis=0, concat_axis=0, tiled=True)
        states.append(jnp.transpose(state, (1, 0, 2)))
        outs.append(jnp.transpose(unpack(home, slot_dev), (1, 2, 0)))
    spec_state = jnp.transpose(jnp.concatenate(states, axis=0), (1, 2, 0))
    new_rows = jnp.transpose(jnp.concatenate(outs, axis=0), (1, 2, 0))
    return (spec_state, new_rows)


def solution(mesh):
    in_specs = (
        P(("grp", "wave"), None, None),
        P(("grp", "wave"), None, None),
        P(),
        P(),
        P("wave", None, None),
        P(),
        P(),
        P(),
    )
    out_specs = (P(("grp", "wave"), None, None), P(("grp", "wave"), None, None))
    return jax.shard_map(
        per_device, mesh=mesh, in_specs=in_specs, out_specs=out_specs, check_vma=False
    )
```

```python
import functools

import jax
import jax.numpy as jnp
from jax import lax
from jax.experimental import pallas as pl
from jax.experimental.pallas import tpu as pltpu
from jax.sharding import PartitionSpec as P

NMAX = 2559
VMEM_LIMIT = 60 * 1024 * 1024
STEP = 16


def pack_kernel(own, counts_ref, waves_ref, north_ref, south_ref, out_ref, turned):
    lats = north_ref.shape[2]
    live = 2 * waves_ref[...] < counts_ref[...]
    total = north_ref[0].astype(jnp.float32) + south_ref[0].astype(jnp.float32)
    turned[...] = jnp.swapaxes(jnp.where(live[None], total, 0.0), 1, 2)
    for d in range(out_ref.shape[0]):
        for i in range(own):
            rows = turned[:, own * d + i, :].astype(jnp.bfloat16)
            out_ref[d, :, lats * i : lats * (i + 1)] = rows


def pack(part, own, north, south, counts, waves):
    _, levels, lats, slots = north.shape
    rows = pl.BlockSpec((1, STEP, lats, slots), lambda g: (part, g, 0, 0))
    return pl.pallas_call(
        functools.partial(pack_kernel, own),
        grid=(pl.cdiv(levels, STEP),),
        in_specs=[
            pl.BlockSpec((lats, 1), lambda g: (0, 0)),
            pl.BlockSpec((1, slots), lambda g: (0, 0)),
            rows,
            rows,
        ],
        out_specs=pl.BlockSpec((slots // own, STEP, own * lats), lambda g: (0, g, 0)),
        out_shape=jax.ShapeDtypeStruct((slots // own, levels, own * lats), jnp.bfloat16),
        scratch_shapes=[pltpu.VMEM((STEP, slots, lats), jnp.float32)],
        cost_estimate=pl.CostEstimate(flops=0, bytes_accessed=levels * lats * slots * 6, transcendentals=0),
        name=f"pack{part}",
    )(counts, waves, north, south)


def unpack_kernel(own, in_ref, *refs):
    out_ref, turned = refs[-2:]
    lats = out_ref.shape[2]
    for d in range(in_ref.shape[0]):
        for i in range(own):
            rows = in_ref[d, :, lats * i : lats * (i + 1)]
            turned[:, own * d + i, :] = rows.astype(jnp.float32)
    out_ref[0] = jnp.swapaxes(turned[...], 1, 2).astype(jnp.bfloat16)


def unpack(part, own, packed, placed):
    senders, levels, width = packed.shape
    lats, slots = width // own, senders * own
    in_specs = [pl.BlockSpec((senders, STEP, width), lambda g: (0, g, 0))]
    operands = [packed]
    aliases = {}
    if placed is not None:
        in_specs.append(pl.BlockSpec(memory_space=pl.ANY))
        operands.append(placed)
        aliases = {1: 0}
    return pl.pallas_call(
        functools.partial(unpack_kernel, own),
        grid=(pl.cdiv(levels, STEP),),
        in_specs=in_specs,
        out_specs=pl.BlockSpec((1, STEP, lats, slots), lambda g: (part, g, 0, 0)),
        out_shape=jax.ShapeDtypeStruct((2, levels, lats, slots), jnp.bfloat16),
        scratch_shapes=[pltpu.VMEM((STEP, slots, lats), jnp.float32)],
        input_output_aliases=aliases,
        cost_estimate=pl.CostEstimate(flops=0, bytes_accessed=levels * lats * slots * 4, transcendentals=0),
        name=f"unpack{part}",
    )(*operands)


def compute_kernel(
    own, senders, lats, waves_ref, counts_ref, rates_ref, to_ref, from_ref, rows_ref, leg_ref,
    state_ref, back_ref, columns, returned,
):
    slot = pl.program_id(0)

    @pl.when(slot == 0)
    def _():
        for s in range(own):
            for d in range(senders):
                columns[s, :, lats * d : lats * (d + 1)] = rows_ref[d, :, lats * s : lats * (s + 1)]

    wave = waves_ref[slot]
    direct = lax.dot_general(
        columns[slot], leg_ref[0], (((1,), (1,)), ((), ())), preferred_element_type=jnp.float32
    ).astype(jnp.bfloat16)
    modal = jnp.dot(to_ref[...], direct, preferred_element_type=jnp.float32)
    degree = wave + 2 * lax.broadcasted_iota(jnp.int32, (1, leg_ref.shape[1]), 1)
    degree_f = degree.astype(jnp.float32)
    scaled_degree = degree_f * (degree_f + 1.0) / float(NMAX * (NMAX + 1))
    divisor = 1.0 + rates_ref[...] * scaled_degree
    scaled = (modal / divisor).astype(jnp.bfloat16)
    state = jnp.dot(from_ref[...], scaled, preferred_element_type=jnp.float32)
    state = jnp.where(degree <= NMAX, state, 0.0).astype(jnp.bfloat16)
    state_ref[0] = state
    back = jnp.dot(state, leg_ref[0], preferred_element_type=jnp.float32)
    returned[slot] = jnp.where(2 * wave < counts_ref[...], back, 0.0).astype(jnp.bfloat16)

    @pl.when(slot == own - 1)
    def _():
        for s in range(own):
            for d in range(senders):
                back_ref[d, :, lats * s : lats * (s + 1)] = returned[s, :, lats * d : lats * (d + 1)]


def compute(rows, legendre, own_waves, counts, rates, to_t, from_t):
    senders, levels, width = rows.shape
    own, row_total, lat_total = legendre.shape
    lats = lat_total // senders
    whole = lambda *shape: pl.BlockSpec(shape, lambda s, w: (0,) * len(shape))
    return pl.pallas_call(
        functools.partial(compute_kernel, own, senders, lats),
        grid_spec=pltpu.PrefetchScalarGridSpec(
            num_scalar_prefetch=1,
            grid=(own,),
            in_specs=[
                whole(1, lat_total),
                whole(levels, 1),
                whole(levels, levels),
                whole(levels, levels),
                whole(senders, levels, width),
                pl.BlockSpec((1, row_total, lat_total), lambda s, w: (s, 0, 0)),
            ],
            out_specs=[
                pl.BlockSpec((1, levels, row_total), lambda s, w: (s, 0, 0)),
                whole(senders, levels, width),
            ],
            scratch_shapes=[
                pltpu.VMEM((own, levels, lat_total), jnp.bfloat16),
                pltpu.VMEM((own, levels, lat_total), jnp.bfloat16),
            ],
        ),
        out_shape=[
            jax.ShapeDtypeStruct((own, levels, row_total), jnp.bfloat16),
            jax.ShapeDtypeStruct((senders, levels, width), jnp.bfloat16),
        ],
        compiler_params=pltpu.CompilerParams(vmem_limit_bytes=VMEM_LIMIT),
        cost_estimate=pl.CostEstimate(
            flops=8 * own * row_total * lat_total * levels,
            bytes_accessed=2 * own * row_total * lat_total,
            transcendentals=0,
        ),
        name="legendre",
    )(own_waves, counts, rates, to_t, from_t, rows, legendre)


def per_device(
    north_rows, south_rows, lon_counts, slot_wave, legendre, mode_rates, to_modes, from_modes
):
    lat_dev = north_rows.shape[0]
    slot_dev, row_total, lat_total = legendre.shape
    levels = to_modes.shape[0]
    my_index = lax.axis_index("wave")
    own_waves = lax.dynamic_slice_in_dim(slot_wave, my_index * slot_dev, slot_dev)
    local_counts = lax.dynamic_slice_in_dim(lon_counts, my_index * lat_dev, lat_dev)
    slots = slot_wave.shape[0]
    north = jnp.transpose(north_rows, (2, 0, 1)).reshape(2, levels, lat_dev, slots)
    south = jnp.transpose(south_rows, (2, 0, 1)).reshape(2, levels, lat_dev, slots)
    counts_here, waves_all = local_counts[:, None], slot_wave[None, :]
    counts_all, rates = lon_counts[None, :], mode_rates[:, None]
    to_t, from_t = to_modes.T, from_modes.T
    states, placed = [], None
    for part in range(2):
        packed = pack(part, slot_dev, north, south, counts_here, waves_all)
        moved = lax.all_to_all(packed, "wave", split_axis=0, concat_axis=0, tiled=True)
        state, back = compute(moved, legendre, own_waves, counts_all, rates, to_t, from_t)
        home = lax.all_to_all(back, "wave", split_axis=0, concat_axis=0, tiled=True)
        states.append(jnp.transpose(state, (1, 0, 2)))
        placed = unpack(part, slot_dev, home, placed)
    spec_state = jnp.transpose(jnp.concatenate(states, axis=0), (1, 2, 0))
    new_rows = jnp.transpose(placed.reshape(2 * levels, lat_dev, slots), (1, 2, 0))
    return (spec_state, new_rows)


def solution(mesh):
    in_specs = (
        P(("grp", "wave"), None, None),
        P(("grp", "wave"), None, None),
        P(),
        P(),
        P("wave", None, None),
        P(),
        P(),
        P(),
    )
    out_specs = (P(("grp", "wave"), None, None), P(("grp", "wave"), None, None))
    return jax.shard_map(
        per_device, mesh=mesh, in_specs=in_specs, out_specs=out_specs, check_vma=False
    )
```

```python
import functools

import jax
import jax.numpy as jnp
from jax import lax
from jax.experimental import pallas as pl
from jax.experimental.pallas import tpu as pltpu
from jax.sharding import PartitionSpec as P

NMAX = 2559
VMEM_LIMIT = 60 * 1024 * 1024
STEP = 16
UNPACK_STEP = 24


def pack_kernel(own, counts_ref, waves_ref, north_ref, south_ref, out_ref, turned):
    lats = north_ref.shape[2]
    live = 2 * waves_ref[...] < counts_ref[...]
    total = north_ref[0].astype(jnp.float32) + south_ref[0].astype(jnp.float32)
    kept = jnp.where(live[None], total, 0.0).astype(jnp.bfloat16)
    turned[...] = jnp.swapaxes(kept, 1, 2).astype(jnp.float32)
    for d in range(out_ref.shape[0]):
        for i in range(own):
            rows = turned[:, own * d + i, :].astype(jnp.bfloat16)
            out_ref[d, :, lats * i : lats * (i + 1)] = rows


def pack(part, own, north, south, counts, waves):
    _, levels, lats, slots = north.shape
    rows = pl.BlockSpec((1, STEP, lats, slots), lambda g: (part, g, 0, 0))
    return pl.pallas_call(
        functools.partial(pack_kernel, own),
        grid=(pl.cdiv(levels, STEP),),
        in_specs=[
            pl.BlockSpec((lats, 1), lambda g: (0, 0)),
            pl.BlockSpec((1, slots), lambda g: (0, 0)),
            rows,
            rows,
        ],
        out_specs=pl.BlockSpec((slots // own, STEP, own * lats), lambda g: (0, g, 0)),
        out_shape=jax.ShapeDtypeStruct((slots // own, levels, own * lats), jnp.bfloat16),
        scratch_shapes=[pltpu.VMEM((STEP, slots, lats), jnp.float32)],
        cost_estimate=pl.CostEstimate(flops=0, bytes_accessed=levels * lats * slots * 6, transcendentals=0),
        name=f"pack{part}",
    )(counts, waves, north, south)


def unpack_kernel(own, in_ref, *refs):
    out_ref, turned = refs[-2:]
    lats = out_ref.shape[2]
    for d in range(in_ref.shape[0]):
        for i in range(own):
            rows = in_ref[d, :, lats * i : lats * (i + 1)]
            turned[own * d + i] = rows.astype(jnp.float32)
    for c in range(out_ref.shape[1]):
        out_ref[0, c] = turned[:, c, :].T.astype(jnp.bfloat16)


def unpack(part, own, packed, placed):
    senders, levels, width = packed.shape
    lats, slots = width // own, senders * own
    in_specs = [pl.BlockSpec((senders, UNPACK_STEP, width), lambda g: (0, g, 0))]
    operands = [packed]
    aliases = {}
    if placed is not None:
        in_specs.append(pl.BlockSpec(memory_space=pl.ANY))
        operands.append(placed)
        aliases = {1: 0}
    return pl.pallas_call(
        functools.partial(unpack_kernel, own),
        grid=(pl.cdiv(levels, UNPACK_STEP),),
        in_specs=in_specs,
        out_specs=pl.BlockSpec((1, UNPACK_STEP, lats, slots), lambda g: (part, g, 0, 0)),
        out_shape=jax.ShapeDtypeStruct((2, levels, lats, slots), jnp.bfloat16),
        scratch_shapes=[pltpu.VMEM((slots, UNPACK_STEP, lats), jnp.float32)],
        input_output_aliases=aliases,
        cost_estimate=pl.CostEstimate(flops=0, bytes_accessed=levels * lats * slots * 4, transcendentals=0),
        name=f"unpack{part}",
    )(*operands)


def compute_kernel(
    own, senders, lats, waves_ref, counts_ref, rates_ref, to_ref, from_ref, rows_ref, leg_ref,
    state_ref, back_ref, columns, returned,
):
    slot = pl.program_id(0)

    @pl.when(slot == 0)
    def _():
        for s in range(own):
            for d in range(senders):
                columns[s, :, lats * d : lats * (d + 1)] = rows_ref[d, :, lats * s : lats * (s + 1)]

    wave = waves_ref[slot]
    direct = lax.dot_general(
        columns[slot], leg_ref[0], (((1,), (1,)), ((), ())), preferred_element_type=jnp.float32
    ).astype(jnp.bfloat16)
    modal = jnp.dot(to_ref[...], direct, preferred_element_type=jnp.float32)
    degree = wave + 2 * lax.broadcasted_iota(jnp.int32, (1, leg_ref.shape[1]), 1)
    degree_f = degree.astype(jnp.float32)
    scaled_degree = degree_f * (degree_f + 1.0) / float(NMAX * (NMAX + 1))
    divisor = 1.0 + rates_ref[...] * scaled_degree
    scaled = (modal / divisor).astype(jnp.bfloat16)
    state = jnp.dot(from_ref[...], scaled, preferred_element_type=jnp.float32)
    state = jnp.where(degree <= NMAX, state, 0.0).astype(jnp.bfloat16)
    state_ref[0] = state
    back = jnp.dot(state, leg_ref[0], preferred_element_type=jnp.float32)
    returned[slot] = jnp.where(2 * wave < counts_ref[...], back, 0.0).astype(jnp.bfloat16)

    @pl.when(slot == own - 1)
    def _():
        for s in range(own):
            for d in range(senders):
                back_ref[d, :, lats * s : lats * (s + 1)] = returned[s, :, lats * d : lats * (d + 1)]


def compute(rows, legendre, own_waves, counts, rates, to_t, from_t):
    senders, levels, width = rows.shape
    own, row_total, lat_total = legendre.shape
    lats = lat_total // senders
    whole = lambda *shape: pl.BlockSpec(shape, lambda s, w: (0,) * len(shape))
    return pl.pallas_call(
        functools.partial(compute_kernel, own, senders, lats),
        grid_spec=pltpu.PrefetchScalarGridSpec(
            num_scalar_prefetch=1,
            grid=(own,),
            in_specs=[
                whole(1, lat_total),
                whole(levels, 1),
                whole(levels, levels),
                whole(levels, levels),
                whole(senders, levels, width),
                pl.BlockSpec((1, row_total, lat_total), lambda s, w: (s, 0, 0)),
            ],
            out_specs=[
                pl.BlockSpec((1, levels, row_total), lambda s, w: (s, 0, 0)),
                whole(senders, levels, width),
            ],
            scratch_shapes=[
                pltpu.VMEM((own, levels, lat_total), jnp.bfloat16),
                pltpu.VMEM((own, levels, lat_total), jnp.bfloat16),
            ],
        ),
        out_shape=[
            jax.ShapeDtypeStruct((own, levels, row_total), jnp.bfloat16),
            jax.ShapeDtypeStruct((senders, levels, width), jnp.bfloat16),
        ],
        compiler_params=pltpu.CompilerParams(vmem_limit_bytes=VMEM_LIMIT),
        cost_estimate=pl.CostEstimate(
            flops=8 * own * row_total * lat_total * levels,
            bytes_accessed=2 * own * row_total * lat_total,
            transcendentals=0,
        ),
        name="legendre",
    )(own_waves, counts, rates, to_t, from_t, rows, legendre)


def per_device(
    north_rows, south_rows, lon_counts, slot_wave, legendre, mode_rates, to_modes, from_modes
):
    lat_dev = north_rows.shape[0]
    slot_dev, row_total, lat_total = legendre.shape
    levels = to_modes.shape[0]
    my_index = lax.axis_index("wave")
    own_waves = lax.dynamic_slice_in_dim(slot_wave, my_index * slot_dev, slot_dev)
    local_counts = lax.dynamic_slice_in_dim(lon_counts, my_index * lat_dev, lat_dev)
    slots = slot_wave.shape[0]
    north = jnp.transpose(north_rows, (2, 0, 1)).reshape(2, levels, lat_dev, slots)
    south = jnp.transpose(south_rows, (2, 0, 1)).reshape(2, levels, lat_dev, slots)
    counts_here, waves_all = local_counts[:, None], slot_wave[None, :]
    counts_all, rates = lon_counts[None, :], mode_rates[:, None]
    to_t, from_t = to_modes.T, from_modes.T
    states, placed = [], None
    for part in range(2):
        packed = pack(part, slot_dev, north, south, counts_here, waves_all)
        moved = lax.all_to_all(packed, "wave", split_axis=0, concat_axis=0, tiled=True)
        state, back = compute(moved, legendre, own_waves, counts_all, rates, to_t, from_t)
        home = lax.all_to_all(back, "wave", split_axis=0, concat_axis=0, tiled=True)
        states.append(jnp.transpose(state, (1, 0, 2)))
        placed = unpack(part, slot_dev, home, placed)
    spec_state = jnp.transpose(jnp.concatenate(states, axis=0), (1, 2, 0))
    new_rows = jnp.transpose(placed.reshape(2 * levels, lat_dev, slots), (1, 2, 0))
    return (spec_state, new_rows)


def solution(mesh):
    in_specs = (
        P(("grp", "wave"), None, None),
        P(("grp", "wave"), None, None),
        P(),
        P(),
        P("wave", None, None),
        P(),
        P(),
        P(),
    )
    out_specs = (P(("grp", "wave"), None, None), P(("grp", "wave"), None, None))
    return jax.shard_map(
        per_device, mesh=mesh, in_specs=in_specs, out_specs=out_specs, check_vma=False
    )
```

```python
import functools

import jax
import jax.numpy as jnp
from jax import lax
from jax.experimental import pallas as pl
from jax.experimental.pallas import tpu as pltpu
from jax.sharding import PartitionSpec as P

NMAX = 2559
VMEM_LIMIT = 60 * 1024 * 1024
STEP = 16
UNPACK_STEP = 24


def pack_kernel(own, counts_ref, waves_ref, north_ref, south_ref, out_ref, turned):
    lats = north_ref.shape[1]
    live = 2 * waves_ref[...] < counts_ref[...]
    total = north_ref[...].astype(jnp.float32) + south_ref[...].astype(jnp.float32)
    kept = jnp.where(live[None], total, 0.0).astype(jnp.bfloat16)
    turned[...] = jnp.swapaxes(kept, 1, 2).astype(jnp.float32)
    for d in range(out_ref.shape[0]):
        for i in range(own):
            rows = turned[:, own * d + i, :].astype(jnp.bfloat16)
            out_ref[d, :, lats * i : lats * (i + 1)] = rows


def pack(part, own, first, levels, north, south, counts, waves):
    _, lats, slots = north.shape
    start = first // STEP
    rows = pl.BlockSpec((STEP, lats, slots), lambda g: (start + g, 0, 0))
    return pl.pallas_call(
        functools.partial(pack_kernel, own),
        grid=(pl.cdiv(levels, STEP),),
        in_specs=[
            pl.BlockSpec((lats, 1), lambda g: (0, 0)),
            pl.BlockSpec((1, slots), lambda g: (0, 0)),
            rows,
            rows,
        ],
        out_specs=pl.BlockSpec((slots // own, STEP, own * lats), lambda g: (0, g, 0)),
        out_shape=jax.ShapeDtypeStruct((slots // own, levels, own * lats), jnp.bfloat16),
        scratch_shapes=[pltpu.VMEM((STEP, slots, lats), jnp.float32)],
        cost_estimate=pl.CostEstimate(flops=0, bytes_accessed=levels * lats * slots * 6, transcendentals=0),
        name=f"pack{part}",
    )(counts, waves, north, south)


def unpack_kernel(own, in_ref, *refs):
    out_ref, turned = refs[-2:]
    lats = out_ref.shape[2]
    for d in range(in_ref.shape[0]):
        for i in range(own):
            rows = in_ref[d, :, lats * i : lats * (i + 1)]
            turned[own * d + i] = rows.astype(jnp.float32)
    for c in range(out_ref.shape[1]):
        out_ref[0, c] = turned[:, c, :].T.astype(jnp.bfloat16)


def unpack(part, own, packed, placed):
    senders, levels, width = packed.shape
    lats, slots = width // own, senders * own
    in_specs = [pl.BlockSpec((senders, UNPACK_STEP, width), lambda g: (0, g, 0))]
    operands = [packed]
    aliases = {}
    if placed is not None:
        in_specs.append(pl.BlockSpec(memory_space=pl.ANY))
        operands.append(placed)
        aliases = {1: 0}
    return pl.pallas_call(
        functools.partial(unpack_kernel, own),
        grid=(pl.cdiv(levels, UNPACK_STEP),),
        in_specs=in_specs,
        out_specs=pl.BlockSpec((1, UNPACK_STEP, lats, slots), lambda g: (part, g, 0, 0)),
        out_shape=jax.ShapeDtypeStruct((2, levels, lats, slots), jnp.bfloat16),
        scratch_shapes=[pltpu.VMEM((slots, UNPACK_STEP, lats), jnp.float32)],
        input_output_aliases=aliases,
        cost_estimate=pl.CostEstimate(flops=0, bytes_accessed=levels * lats * slots * 4, transcendentals=0),
        name=f"unpack{part}",
    )(*operands)


def compute_kernel(
    own, senders, lats, takes, waves_ref, counts_ref, rates_ref, to_ref, from_ref, leg_ref,
    *refs,
):
    *pieces, state_ref, back_ref, columns, returned = refs
    slot = pl.program_id(0)

    @pl.when(slot == 0)
    def _():
        for s in range(own):
            for d in range(senders):
                lanes = slice(lats * d, lats * (d + 1))
                done = 0
                for (skip, count), rows_ref in zip(takes, pieces):
                    piece = rows_ref[d, skip : skip + count, lats * s : lats * (s + 1)]
                    columns[s, done : done + count, lanes] = piece
                    done += count

    wave = waves_ref[slot]
    direct = lax.dot_general(
        columns[slot], leg_ref[0], (((1,), (1,)), ((), ())), preferred_element_type=jnp.float32
    ).astype(jnp.bfloat16)
    modal = jnp.dot(to_ref[...], direct, preferred_element_type=jnp.float32)
    degree = wave + 2 * lax.broadcasted_iota(jnp.int32, (1, leg_ref.shape[1]), 1)
    degree_f = degree.astype(jnp.float32)
    scaled_degree = degree_f * (degree_f + 1.0) / float(NMAX * (NMAX + 1))
    divisor = 1.0 + rates_ref[...] * scaled_degree
    scaled = (modal / divisor).astype(jnp.bfloat16)
    state = jnp.dot(from_ref[...], scaled, preferred_element_type=jnp.float32)
    state = jnp.where(degree <= NMAX, state, 0.0).astype(jnp.bfloat16)
    state_ref[0] = state
    back = jnp.dot(state, leg_ref[0], preferred_element_type=jnp.float32)
    returned[slot] = jnp.where(2 * wave < counts_ref[...], back, 0.0).astype(jnp.bfloat16)

    @pl.when(slot == own - 1)
    def _():
        for s in range(own):
            for d in range(senders):
                back_ref[d, :, lats * s : lats * (s + 1)] = returned[s, :, lats * d : lats * (d + 1)]


def compute(rows, takes, legendre, own_waves, counts, rates, to_t, from_t):
    senders, _, width = rows[0].shape
    levels = to_t.shape[0]
    own, row_total, lat_total = legendre.shape
    lats = lat_total // senders
    whole = lambda *shape: pl.BlockSpec(shape, lambda s, w: (0,) * len(shape))
    return pl.pallas_call(
        functools.partial(compute_kernel, own, senders, lats, takes),
        grid_spec=pltpu.PrefetchScalarGridSpec(
            num_scalar_prefetch=1,
            grid=(own,),
            in_specs=[
                whole(1, lat_total),
                whole(levels, 1),
                whole(levels, levels),
                whole(levels, levels),
                pl.BlockSpec((1, row_total, lat_total), lambda s, w: (s, 0, 0)),
                *[whole(*piece.shape) for piece in rows],
            ],
            out_specs=[
                pl.BlockSpec((1, levels, row_total), lambda s, w: (s, 0, 0)),
                whole(senders, levels, width),
            ],
            scratch_shapes=[
                pltpu.VMEM((own, levels, lat_total), jnp.bfloat16),
                pltpu.VMEM((own, levels, lat_total), jnp.bfloat16),
            ],
        ),
        out_shape=[
            jax.ShapeDtypeStruct((own, levels, row_total), jnp.bfloat16),
            jax.ShapeDtypeStruct((senders, levels, width), jnp.bfloat16),
        ],
        compiler_params=pltpu.CompilerParams(vmem_limit_bytes=VMEM_LIMIT),
        cost_estimate=pl.CostEstimate(
            flops=8 * own * row_total * lat_total * levels,
            bytes_accessed=2 * own * row_total * lat_total,
            transcendentals=0,
        ),
        name="legendre",
    )(own_waves, counts, rates, to_t, from_t, legendre, *rows)


def per_device(
    north_rows, south_rows, lon_counts, slot_wave, legendre, mode_rates, to_modes, from_modes
):
    lat_dev = north_rows.shape[0]
    slot_dev, row_total, lat_total = legendre.shape
    levels = to_modes.shape[0]
    my_index = lax.axis_index("wave")
    own_waves = lax.dynamic_slice_in_dim(slot_wave, my_index * slot_dev, slot_dev)
    local_counts = lax.dynamic_slice_in_dim(lon_counts, my_index * lat_dev, lat_dev)
    slots = slot_wave.shape[0]
    north = jnp.transpose(north_rows, (2, 0, 1))
    south = jnp.transpose(south_rows, (2, 0, 1))
    counts_here, waves_all = local_counts[:, None], slot_wave[None, :]
    counts_all, rates = lon_counts[None, :], mode_rates[:, None]
    to_t, from_t = to_modes.T, from_modes.T
    head = pl.cdiv(levels, STEP) * STEP
    moved, states, placed = [], [], None
    for part, (first, count) in enumerate(((0, head), (head, 2 * levels - head))):
        packed = pack(part, slot_dev, first, count, north, south, counts_here, waves_all)
        moved.append(lax.all_to_all(packed, "wave", split_axis=0, concat_axis=0, tiled=True))
    cuts = (
        (moved[:1], ((0, levels),)),
        (moved, ((levels, head - levels), (0, 2 * levels - head))),
    )
    for part, (rows, takes) in enumerate(cuts):
        state, back = compute(
            rows, takes, legendre, own_waves, counts_all, rates, to_t, from_t
        )
        home = lax.all_to_all(back, "wave", split_axis=0, concat_axis=0, tiled=True)
        states.append(jnp.transpose(state, (1, 0, 2)))
        placed = unpack(part, slot_dev, home, placed)
    spec_state = jnp.transpose(jnp.concatenate(states, axis=0), (1, 2, 0))
    new_rows = jnp.transpose(placed.reshape(2 * levels, lat_dev, slots), (1, 2, 0))
    return (spec_state, new_rows)


def solution(mesh):
    in_specs = (
        P(("grp", "wave"), None, None),
        P(("grp", "wave"), None, None),
        P(),
        P(),
        P("wave", None, None),
        P(),
        P(),
        P(),
    )
    out_specs = (P(("grp", "wave"), None, None), P(("grp", "wave"), None, None))
    return jax.shard_map(
        per_device, mesh=mesh, in_specs=in_specs, out_specs=out_specs, check_vma=False
    )
```
